32 devices in a mesh: row: 4 (over y, core), col: 8 (over z, x).
Axes of the slice: x: 2, y: 2, z: 4, core: 2. Of those that a mesh axis runs over, the one named last changes fastest.
Arguments:
- constraint_blocks: float32 [16, 16, 256, 256], P('row', 'col'), may hold values from -0.09375 to 0.09375
- factor_blocks: float32 [16, 16, 256, 256], P('row', 'col'), may hold values from -0.09375 to 0.09375
- band_offsets: int32 [8, 2], P('col'), may hold values from 0 to 63, as said below
- block_pattern: int32 [16, 16], P('row', 'col'), may hold values 0 or 1
- cost_linear: float32 [131072], P('col'), may hold values from -6 to 6
- cost_diagonal: float32 [131072], P('col'), may hold values from 0.5 to 4
- lower: float32 [4096], P('row'), may hold values from -1.5 to -0.2
- upper: float32 [4096], P('row'), may hold values from 0.2 to 1.5
- x_start: float32 [131072], P('col'), may hold values from -6 to 6
- z_start: float32 [4096], P('row'), may hold values from -1 to 1
- y_start: float32 [4096], P('row'), may hold values from -0.6 to 0.6
Outputs:
- x_final: float32 [131072], P('col')
- z_final: float32 [4096], P('row')
- y_final: float32 [4096], P('row')
- residuals: float32 [2, 2], replicated
The draws below stay inside these ranges and needn't reach their ends.
Inputs may be any that keep to these rules, and one draw needn't show every extreme that they name: In each row of band_offsets the 2 offsets are distinct.
All inputs are finite; a program needn't handle non-finite values. No bound on the sum of `block_pattern` on one device may be relied on, other than what follows from the above.
Results may differ from the reference program's by a relative error of at most 0.00016.
Values sent between devices are 32-bit elements; how exact they have to be, the bound alone decides.
A program may use at most 64 MiB of HBM per device.

```python
import math
import jax
import jax.numpy as jnp
from jax import lax

BS = 256
KB = 2
CBD = 64
ITERS = 2
CG_STEPS = 2
GROUPS = 8
BANDS = 16
NBR = 16
NBC = 512
MROWS = 4096
NVARS = 131072


def draw_band_offsets(key, part):
    keys = jax.random.split(jax.random.fold_in(key, 17), GROUPS)

    def one_group(group_key):
        return jax.random.permutation(group_key, CBD)[:KB].astype(jnp.int32)
    return jax.vmap(one_group)(keys).astype(jnp.int32)


def set_ends(array, stream_key, low, largest):
    dims = array.shape
    place = [jax.random.randint(jax.random.fold_in(stream_key, axis), (), 0, dims[axis]) for axis in range(len(dims))]
    array = array.at[tuple(place)].set(low)
    longest = dims.index(max(dims))
    place[longest] = (place[longest] + 1) % dims[longest]
    return array.at[tuple(place)].set(largest)


def levels(own_key, dims, cuts, smallest, top_value):
    def one(axis_at, parts):
        heights = jax.random.uniform(jax.random.fold_in(jax.random.fold_in(own_key, 6), axis_at), (parts,), jnp.float32, smallest / len(cuts), top_value / len(cuts))
        return jnp.repeat(jnp.exp(heights), dims[axis_at] // parts).reshape((-1,) + (1,) * (len(dims) - axis_at - 1))

    level = one(*cuts[0])
    for cut in cuts[1:]:
        level = level * one(*cut)
    return level


def normal_values(stream_key, dims, spread, bound, cuts=(), kind=jnp.bfloat16):
    factor_of = levels(stream_key, dims, cuts, -0.22, 0.18) if cuts else 1.0
    array = jax.random.normal(stream_key, dims, jnp.float32) * spread * factor_of
    return jnp.minimum(jnp.maximum(array, -bound), bound).astype(kind)


def setup_inputs(seed: int = 0) -> dict:
    splits = jax.random.split(jax.random.key(seed), 12)
    constraint_blocks = normal_values(splits[0], (NBR, BANDS, BS, BS), (BANDS * BS) ** -0.5, 0.09375, ((0, 4), (1, 8)), jnp.float32)
    factor_blocks = normal_values(splits[1], (NBR, BANDS, BS, BS), (BANDS * BS) ** -0.5, 0.09375, ((0, 4), (1, 8)), jnp.float32)
    band_offsets = draw_band_offsets(jax.random.fold_in(splits[11], 71), 0)
    block_pattern = set_ends((jax.random.randint(splits[3], (NBR, BANDS), 0, 4) < 3).astype(jnp.int32), jax.random.fold_in(splits[3], 1), 0, 1)
    cost_linear = normal_values(splits[4], (NVARS,), 1.0, 6.0, ((0, 8),), jnp.float32)
    cost_diagonal = jnp.clip(jnp.exp(math.log(4.0) - 2.0794415 * jax.random.uniform(splits[5], (NVARS,), jnp.float32) ** levels(splits[5], (NVARS,), ((0, 8),), -0.2, 0.2)), 0.5, 4.0)
    lower = jnp.clip(-1.5 + 1.3 * jax.random.uniform(splits[6], (MROWS,), jnp.float32) ** levels(splits[6], (MROWS,), ((0, 4),), -0.2, 0.2), -1.5, -0.2)
    upper = jnp.clip(0.2 + 1.3 * jax.random.uniform(splits[7], (MROWS,), jnp.float32) ** levels(splits[7], (MROWS,), ((0, 4),), -0.2, 0.2), 0.2, 1.5)
    x_start = normal_values(splits[8], (NVARS,), 1.0, 6.0, ((0, 8),), jnp.float32)
    z_start = jnp.clip(jax.random.uniform(splits[9], (MROWS,), jnp.float32, -1.0, 1.0) * levels(splits[9], (MROWS,), ((0, 4),), -0.4, 0.0), -1.0, 1.0)
    y_start = normal_values(splits[10], (MROWS,), 0.1, 0.6, ((0, 4),), jnp.float32)
    return {"constraint_blocks": constraint_blocks, "factor_blocks": factor_blocks, "band_offsets": band_offsets, "block_pattern": block_pattern, "cost_linear": cost_linear, "cost_diagonal": cost_diagonal, "lower": lower, "upper": upper, "x_start": x_start, "z_start": z_start, "y_start": y_start}


sigma_shift = 1e-6
rho_step = 0.1
relaxation = 1.6


def column_map(band_offsets):
    block_rows = jnp.arange(NBR, dtype=jnp.int32)
    group_ids = jnp.arange(GROUPS, dtype=jnp.int32)
    inner = (block_rows[:, None, None] % CBD + band_offsets[None, :, :]) % CBD
    columns = group_ids[None, :, None] * CBD + inner
    return columns.reshape(NBR, BANDS).astype(jnp.int32)


def forward(blocks, pattern, columns, vector):
    vector_blocks = vector.reshape(NBC, BS)
    gathered = vector_blocks[columns] * pattern[:, :, None]
    result = jnp.einsum("ijab,ijb->ia", blocks, gathered, precision=lax.Precision.HIGHEST)
    return result.reshape(-1)


def backward(blocks, pattern, columns, vector):
    vector_blocks = vector.reshape(NBR, BS)
    contrib = jnp.einsum("ijab,ia->ijb", blocks, vector_blocks, precision=lax.Precision.HIGHEST)
    contrib = contrib * pattern[:, :, None]
    summed = jax.ops.segment_sum(contrib.reshape(-1, BS), columns.reshape(-1), num_segments=NBC)
    return summed.reshape(-1)


def reference(constraint_blocks, factor_blocks, band_offsets, block_pattern, cost_linear, cost_diagonal, lower, upper, x_start, z_start, y_start):
    columns = column_map(band_offsets)
    pattern = block_pattern.astype(jnp.float32)
    shifted = cost_diagonal + sigma_shift

    def apply_a(vector):
        return forward(constraint_blocks, pattern, columns, vector)

    def apply_at(vector):
        return backward(constraint_blocks, pattern, columns, vector)

    def apply_gtg(vector):
        return backward(factor_blocks, pattern, columns, forward(factor_blocks, pattern, columns, vector))

    def apply_m(vector):
        return shifted * vector + apply_gtg(vector) + rho_step * apply_at(apply_a(vector))

    iterate, z_value, y_value = x_start, z_start, y_start
    primal_list = []
    dual_list = []
    for outer in range(ITERS):
        rhs = sigma_shift * iterate - cost_linear + apply_at(rho_step * z_value - y_value)
        solved = iterate
        remainder = rhs - apply_m(iterate)
        direction = remainder
        norm_now = jnp.sum(remainder * remainder)
        for inner in range(CG_STEPS):
            image = apply_m(direction)
            step_size = norm_now / jnp.sum(direction * image)
            solved = solved + step_size * direction
            remainder = remainder - step_size * image
            norm_next = jnp.sum(remainder * remainder)
            direction = remainder + (norm_next / norm_now) * direction
            norm_now = norm_next
        z_tilde = apply_a(solved)
        iterate = relaxation * solved + (1.0 - relaxation) * iterate
        blended = relaxation * z_tilde + (1.0 - relaxation) * z_value
        z_new = jnp.minimum(jnp.maximum(blended + y_value / rho_step, lower), upper)
        y_value = y_value + rho_step * (blended - z_new)
        z_value = z_new
        primal_list.append(jnp.max(jnp.abs(apply_a(iterate) - z_value)))
        dual_vec = cost_diagonal * iterate + apply_gtg(iterate) + cost_linear + apply_at(y_value)
        dual_list.append(jnp.max(jnp.abs(dual_vec)))
    residuals = jnp.stack([jnp.stack(primal_list), jnp.stack(dual_list)])
    return iterate, z_value, y_value, residuals
```

```python
import functools

import jax
import jax.numpy as jnp
from jax import lax
from jax.experimental import pallas as pl
from jax.experimental.pallas import tpu as pltpu
from jax.sharding import PartitionSpec as P

ITERS = 2
CG_STEPS = 2
LANES = 128

sigma_shift = 1e-06
rho_step = 0.1
relaxation = 1.6

f32 = jnp.float32
bf16 = jnp.bfloat16


def kernel(
    n_row,
    n_col,
    a_blocks,
    g_blocks,
    offsets,
    pattern,
    q_ref,
    d_ref,
    lower_ref,
    upper_ref,
    x0_ref,
    z0_ref,
    y0_ref,
    x_ref,
    z_ref,
    y_ref,
    res_ref,
    f_hi,
    f_lo,
    r_ref,
    p_ref,
    s_ref,
    wide,
    col_buf,
    row_buf,
    col_send,
    col_recv,
    row_send,
    row_recv,
):
    row_blocks, bands, bs, _ = a_blocks.shape
    halves = bs // LANES
    tile = halves * row_blocks
    length = x0_ref.shape[0]
    col_blocks = length // halves
    my_row = lax.axis_index("row")
    my_col = lax.axis_index("col")

    barrier = pltpu.get_barrier_semaphore()
    for d in range(1, n_row):
        pl.semaphore_signal(barrier, inc=1, device_id={"row": lax.rem(my_row + d, n_row)})
    for d in range(1, n_col):
        pl.semaphore_signal(barrier, inc=1, device_id={"col": lax.rem(my_col + d, n_col)})

    for t in range(row_blocks):
        for k in range(bands):
            on = pattern[t, k].astype(f32)
            for m, blocks in enumerate((g_blocks, a_blocks)):
                value = blocks[t, k] * on
                high = value.astype(bf16)
                f_hi[t, m * bs : (m + 1) * bs, k * bs : (k + 1) * bs] = high
                f_lo[t, m * bs : (m + 1) * bs, k * bs : (k + 1) * bs] = (
                    value - high.astype(f32)
                ).astype(bf16)
    wide[...] = jnp.zeros_like(wide)
    pl.semaphore_wait(barrier, n_row + n_col - 2)

    line = lax.broadcasted_iota(jnp.int32, (8, bands * bs), 0)
    line_y = lax.broadcasted_iota(jnp.int32, (8, 2 * bs), 0)
    sends = []

    def stacked(rows, line):
        total = jnp.zeros(line.shape, f32)
        for i, value in enumerate(rows):
            high = value.astype(bf16).astype(f32)
            total = jnp.where(line == 2 * i, high, total)
            total = jnp.where(line == 2 * i + 1, value - high, total)
        return total.astype(bf16)

    def forward(ref, phase):
        for t in range(row_blocks):
            pieces = []
            for k in range(bands):
                c = lax.rem(my_row * row_blocks + t + offsets[0, k], col_blocks)
                for h in range(halves):
                    pieces.append(ref[pl.ds(c * halves + h, 1), :])
            lhs = stacked([jnp.concatenate(pieces, axis=1)], line)
            dims = (((1,), (1,)), ((), ()))
            out = lax.dot_general(lhs, f_hi[t], dims, preferred_element_type=f32)
            out = out + lax.dot_general(lhs, f_lo[t], dims, preferred_element_type=f32)
            out = out[0:1] + out[1:2]
            for m in range(2):
                for h in range(halves):
                    at = m * bs + h * LANES
                    row = m * tile + t * halves + h
                    col_buf[phase, my_col, row : row + 1, :] = out[:, at : at + LANES]

    def backward(vectors, phase):
        for t in range(row_blocks):
            rows = []
            for g, a in vectors:
                rows.append(
                    jnp.concatenate(
                        [v[t * halves + h : t * halves + h + 1] for v in (g, a) for h in range(halves)],
                        axis=1,
                    )
                )
            lhs = stacked(rows, line_y)
            out = jnp.dot(lhs, f_hi[t], preferred_element_type=f32)
            out = out + jnp.dot(lhs, f_lo[t], preferred_element_type=f32)
            for i in range(len(vectors)):
                value = out[2 * i : 2 * i + 1] + out[2 * i + 1 : 2 * i + 2]
                for k in range(bands):
                    for h in range(halves):
                        at = k * bs + h * LANES
                        row = t * halves + h
                        row_buf[phase, i * bands + k, my_row, row : row + 1, :] = value[
                            :, at : at + LANES
                        ]

    def exchange_col(phase):
        copies = []
        for d in range(1, n_col):
            mine = col_buf.at[phase, my_col]
            copies.append(
                pltpu.make_async_remote_copy(
                    src_ref=mine,
                    dst_ref=mine,
                    send_sem=col_send.at[phase, d],
                    recv_sem=col_recv.at[phase, d],
                    device_id={"col": lax.rem(my_col + d, n_col)},
                )
            )
            copies[-1].start()
        sends.extend(copies)
        for copy in copies:
            copy.wait_recv()

    def exchange_row(phase, first, last):
        copies = []
        for d in range(1, n_row):
            mine = row_buf.at[phase, pl.ds(first, last - first), my_row]
            copies.append(
                pltpu.make_async_remote_copy(
                    src_ref=mine,
                    dst_ref=mine,
                    send_sem=row_send.at[phase, d],
                    recv_sem=row_recv.at[phase, d],
                    device_id={"row": lax.rem(my_row + d, n_row)},
                )
            )
            copies[-1].start()
        sends.extend(copies)
        for copy in copies:
            copy.wait_recv()

    def col_sum(phase):
        total = col_buf[phase, 0]
        for i in range(1, n_col):
            total = total + col_buf[phase, i]
        return total

    extra = bands

    def plane_sum(phase):
        total = row_buf[phase, extra, 0]
        for i in range(1, n_row):
            total = total + row_buf[phase, extra, i]
        return jnp.sum(total, axis=(0, 1), keepdims=True)

    def expand(phase, i):
        total = None
        for k in range(bands):
            at = i * bands + k
            value = row_buf[phase, at].reshape(n_row * tile, LANES)
            wide[at, 0 : n_row * tile, :] = value
            wide[at, length : length + n_row * tile, :] = value
            start = length - halves * offsets[0, k]
            part = wide[at, pl.ds(start, length), :]
            total = part if total is None else total + part
        return total

    def lines(value):
        return jnp.sum(value, axis=0, keepdims=True)

    col_phase = 0
    row_phase = 0
    forward(x0_ref, col_phase)
    col_buf[col_phase, my_col, 2 * tile : 2 * tile + 8, :] = jnp.zeros((8, LANES), f32)
    exchange_col(col_phase)
    total = col_sum(col_phase)
    g, a = total[0:tile], total[tile : 2 * tile]
    col_phase += 1

    z, y = z0_ref[...], y0_ref[...]
    x_ref[...] = x0_ref[...]
    primal, dual = [], []

    def record(dual_sum):
        primal.append(jnp.max(jnp.abs(a - z), axis=0, keepdims=True))
        value = jnp.abs(d_ref[...] * x_ref[...] + q_ref[...] + dual_sum)
        dual.append(jnp.max(value, axis=0, keepdims=True))

    for outer in range(ITERS):
        vectors = [(-g, rho_step * z - y - rho_step * a)]
        if outer > 0:
            vectors.append((g, y))
        backward(vectors, row_phase)
        exchange_row(row_phase, 0, bands * len(vectors))
        start_sum = expand(row_phase, 0)
        if outer > 0:
            record(expand(row_phase, 1))
        row_phase += 1
        x = x_ref[...]
        shifted = d_ref[...] + sigma_shift
        r_ref[...] = sigma_shift * x - q_ref[...] - shifted * x + start_sum
        s_ref[...] = x
        g_s, a_s = g, a
        for inner in range(CG_STEPS):
            r = r_ref[...]
            weighted = (d_ref[...] + sigma_shift) * r
            col_buf[col_phase, my_col, 2 * tile : 2 * tile + 8, :] = jnp.zeros((8, LANES), f32)
            at = 2 * tile
            col_buf[col_phase, my_col, at : at + 1, :] = lines(r * r)
            col_buf[col_phase, my_col, at + 1 : at + 2, :] = lines(weighted * r)
            if inner > 0:
                col_buf[col_phase, my_col, at + 2 : at + 3, :] = lines(weighted * p_ref[...])
            forward(r_ref, col_phase)
            exchange_col(col_phase)
            total = col_sum(col_phase)
            col_phase += 1
            sums = jnp.sum(total[2 * tile : 2 * tile + 8], axis=1, keepdims=True)
            norm, w_rem, w_mix = sums[0:1], sums[1:2], sums[2:3]
            g_r, a_r = total[0:tile], total[tile : 2 * tile]
            if inner == 0:
                p_ref[...] = r
                g_d, a_d, w_dir = g_r, a_r, w_rem
            else:
                ratio = norm / norm_old
                p_ref[...] = r + ratio * p_ref[...]
                g_d = g_r + ratio * g_d
                a_d = a_r + ratio * a_d
                w_dir = w_rem + 2.0 * ratio * w_mix + ratio * ratio * w_dir
            row_buf[row_phase, extra, my_row] = g_d * g_d + rho_step * (a_d * a_d)
            if inner < CG_STEPS - 1:
                backward([(g_d, rho_step * a_d)], row_phase)
                exchange_row(row_phase, 0, extra + 1)
            else:
                exchange_row(row_phase, extra, extra + 1)
            alpha = norm / (plane_sum(row_phase) + w_dir)
            p = p_ref[...]
            s_ref[...] = s_ref[...] + alpha * p
            g_s = g_s + alpha * g_d
            a_s = a_s + alpha * a_d
            if inner < CG_STEPS - 1:
                image = expand(row_phase, 0) + (d_ref[...] + sigma_shift) * p
                r_ref[...] = r_ref[...] - alpha * image
            row_phase += 1
            norm_old = norm
        x_ref[...] = relaxation * s_ref[...] + (1.0 - relaxation) * x_ref[...]
        g = relaxation * g_s + (1.0 - relaxation) * g
        a = relaxation * a_s + (1.0 - relaxation) * a
        blended = relaxation * a_s + (1.0 - relaxation) * z
        z_new = jnp.minimum(jnp.maximum(blended + y / rho_step, lower_ref[...]), upper_ref[...])
        y = y + rho_step * (blended - z_new)
        z = z_new
    z_ref[...] = z
    y_ref[...] = y

    backward([(g, y)], row_phase)
    exchange_row(row_phase, 0, bands)
    record(expand(row_phase, 0))
    row_phase += 1

    found = primal + dual
    row_buf[row_phase, extra, my_row] = jnp.zeros((tile, LANES), f32)
    for i, value in enumerate(found):
        row_buf[row_phase, extra, my_row, i : i + 1, :] = value
    exchange_row(row_phase, extra, extra + 1)
    total = row_buf[row_phase, extra, 0]
    for i in range(1, n_row):
        total = jnp.maximum(total, row_buf[row_phase, extra, i])
    col_buf[col_phase, my_col] = jnp.concatenate([total, total, total], axis=0)
    exchange_col(col_phase)
    total = col_buf[col_phase, 0, 0:tile]
    for i in range(1, n_col):
        total = jnp.maximum(total, col_buf[col_phase, i, 0:tile])
    top = jnp.max(total, axis=1, keepdims=True)
    for i in range(len(found)):
        u, v = divmod(i, ITERS)
        res_ref[u : u + 1, v : v + 1] = top[i : i + 1]
    for copy in sends:
        copy.wait_send()


def solution(mesh):
    n_row, n_col = mesh.shape["row"], mesh.shape["col"]

    def local(a, g, offsets, pattern, q, d, lower, upper, x, z, y):
        row_blocks, bands, bs, _ = a.shape
        tile = row_blocks * bs // LANES
        length = x.shape[0] // LANES
        planes = 2 * bands
        col_phases = 2 + ITERS * CG_STEPS
        row_phases = ITERS * (CG_STEPS + 1) + 2
        flat = lambda v: v.reshape(-1, LANES)
        vmem = pl.BlockSpec(memory_space=pltpu.VMEM)
        smem = pl.BlockSpec(memory_space=pltpu.SMEM)
        out = pl.pallas_call(
            functools.partial(kernel, n_row, n_col),
            name="osqp",
            out_shape=(
                jax.ShapeDtypeStruct((length, LANES), f32),
                jax.ShapeDtypeStruct((tile, LANES), f32),
                jax.ShapeDtypeStruct((tile, LANES), f32),
                jax.ShapeDtypeStruct((2, ITERS), f32),
            ),
            in_specs=[vmem, vmem, smem, smem] + [vmem] * 7,
            out_specs=(vmem, vmem, vmem, vmem),
            scratch_shapes=[
                pltpu.VMEM((row_blocks, 2 * bs, bands * bs), bf16),
                pltpu.VMEM((row_blocks, 2 * bs, bands * bs), bf16),
                pltpu.VMEM((length, LANES), f32),
                pltpu.VMEM((length, LANES), f32),
                pltpu.VMEM((length, LANES), f32),
                pltpu.VMEM((2 * bands, 2 * length, LANES), f32),
                pltpu.VMEM((col_phases, n_col, 2 * tile + 8, LANES), f32),
                pltpu.VMEM((row_phases, planes, n_row, tile, LANES), f32),
                pltpu.SemaphoreType.DMA((col_phases, n_col)),
                pltpu.SemaphoreType.DMA((col_phases, n_col)),
                pltpu.SemaphoreType.DMA((row_phases, n_row)),
                pltpu.SemaphoreType.DMA((row_phases, n_row)),
            ],
            compiler_params=pltpu.CompilerParams(
                collective_id=0, has_side_effects=True, vmem_limit_bytes=48 << 20
            ),
        )(a, g, offsets, pattern, flat(q), flat(d), flat(lower), flat(upper), flat(x), flat(z), flat(y))
        return out[0].reshape(-1), out[1].reshape(-1), out[2].reshape(-1), out[3]

    placed = (
        P("row", "col", None, None),
        P("row", "col", None, None),
        P("col", None),
        P("row", "col"),
        P("col"),
        P("col"),
        P("row"),
        P("row"),
        P("col"),
        P("row"),
        P("row"),
    )
    return jax.shard_map(
        local,
        mesh=mesh,
        in_specs=placed,
        out_specs=(P("col"), P("row"), P("row"), P()),
        check_vma=False,
    )
```

```python
import functools

import jax
import jax.numpy as jnp
from jax import lax
from jax.experimental import pallas as pl
from jax.experimental.pallas import tpu as pltpu
from jax.sharding import PartitionSpec as P

ITERS = 2
CG_STEPS = 2
LANES = 128

sigma_shift = 1e-06
rho_step = 0.1
relaxation = 1.6

f32 = jnp.float32
bf16 = jnp.bfloat16


def kernel(
    n_row,
    n_col,
    a_hbm,
    g_hbm,
    offsets_hbm,
    pattern_hbm,
    q_hbm,
    d_hbm,
    lower_hbm,
    upper_hbm,
    x_hbm,
    z_hbm,
    y_hbm,
    x_ref,
    z_ref,
    y_ref,
    res_ref,
    a_blocks,
    g_blocks,
    offsets,
    pattern,
    q_ref,
    d_ref,
    lower_ref,
    upper_ref,
    block_sem,
    small_sem,
    f_hi,
    f_lo,
    r_ref,
    p_ref,
    s_ref,
    wide,
    col_buf,
    row_buf,
    col_send,
    col_recv,
    row_send,
    row_recv,
):
    row_blocks, bands, bs, _ = a_blocks.shape
    halves = bs // LANES
    tile = halves * row_blocks
    length = x_ref.shape[0]
    col_blocks = length // halves
    my_row = lax.axis_index("row")
    my_col = lax.axis_index("col")

    small = [
        pltpu.make_async_copy(src, dst, small_sem.at[i])
        for i, (src, dst) in enumerate(
            (
                (pattern_hbm, pattern),
                (offsets_hbm, offsets),
                (x_hbm, x_ref),
                (z_hbm, z_ref),
                (y_hbm, y_ref),
                (q_hbm, q_ref),
                (d_hbm, d_ref),
                (lower_hbm, lower_ref),
                (upper_hbm, upper_ref),
            )
        )
    ]
    loads = [
        [
            pltpu.make_async_copy(src.at[t], dst.at[t], block_sem.at[t, m])
            for m, (src, dst) in enumerate(((g_hbm, g_blocks), (a_hbm, a_blocks)))
        ]
        for t in range(row_blocks)
    ]
    for copy in small[:2]:
        copy.start()
    for pair in loads:
        for copy in pair:
            copy.start()
    for copy in small[2:]:
        copy.start()

    barrier = pltpu.get_barrier_semaphore()
    for d in range(1, n_row):
        pl.semaphore_signal(barrier, inc=1, device_id={"row": lax.rem(my_row + d, n_row)})
    for d in range(1, n_col):
        pl.semaphore_signal(barrier, inc=1, device_id={"col": lax.rem(my_col + d, n_col)})

    wide[...] = jnp.zeros_like(wide)
    for copy in small[:2]:
        copy.wait()
    for t in range(row_blocks):
        for copy in loads[t]:
            copy.wait()
        for k in range(bands):
            on = pattern[t, k].astype(f32)
            for m, blocks in enumerate((g_blocks, a_blocks)):
                value = blocks[t, k] * on
                high = value.astype(bf16)
                f_hi[t, m * bs : (m + 1) * bs, k * bs : (k + 1) * bs] = high
                f_lo[t, m * bs : (m + 1) * bs, k * bs : (k + 1) * bs] = (
                    value - high.astype(f32)
                ).astype(bf16)
    for copy in small[2:]:
        copy.wait()
    pl.semaphore_wait(barrier, n_row + n_col - 2)

    line = lax.broadcasted_iota(jnp.int32, (8, bands * bs), 0)
    line_y = lax.broadcasted_iota(jnp.int32, (8, 2 * bs), 0)
    sends = []

    def stacked(rows, line):
        total = jnp.zeros(line.shape, f32)
        for i, value in enumerate(rows):
            high = value.astype(bf16).astype(f32)
            total = jnp.where(line == 2 * i, high, total)
            total = jnp.where(line == 2 * i + 1, value - high, total)
        return total.astype(bf16)

    def forward(ref, phase):
        for t in range(row_blocks):
            pieces = []
            for k in range(bands):
                c = lax.rem(my_row * row_blocks + t + offsets[0, k], col_blocks)
                for h in range(halves):
                    pieces.append(ref[pl.ds(c * halves + h, 1), :])
            lhs = stacked([jnp.concatenate(pieces, axis=1)], line)
            dims = (((1,), (1,)), ((), ()))
            out = lax.dot_general(lhs, f_hi[t], dims, preferred_element_type=f32)
            out = out + lax.dot_general(lhs, f_lo[t], dims, preferred_element_type=f32)
            out = out[0:1] + out[1:2]
            for m in range(2):
                for h in range(halves):
                    at = m * bs + h * LANES
                    row = m * tile + t * halves + h
                    col_buf[phase, my_col, row : row + 1, :] = out[:, at : at + LANES]

    def backward(vectors, phase):
        for t in range(row_blocks):
            rows = []
            for g, a in vectors:
                rows.append(
                    jnp.concatenate(
                        [v[t * halves + h : t * halves + h + 1] for v in (g, a) for h in range(halves)],
                        axis=1,
                    )
                )
            lhs = stacked(rows, line_y)
            out = jnp.dot(lhs, f_hi[t], preferred_element_type=f32)
            out = out + jnp.dot(lhs, f_lo[t], preferred_element_type=f32)
            for i in range(len(vectors)):
                value = out[2 * i : 2 * i + 1] + out[2 * i + 1 : 2 * i + 2]
                for k in range(bands):
                    for h in range(halves):
                        at = k * bs + h * LANES
                        row = t * halves + h
                        row_buf[phase, i * bands + k, my_row, row : row + 1, :] = value[
                            :, at : at + LANES
                        ]

    def exchange_col(phase, rows):
        copies = []
        for d in range(1, n_col):
            mine = col_buf.at[phase, my_col, pl.ds(0, rows)]
            copies.append(
                pltpu.make_async_remote_copy(
                    src_ref=mine,
                    dst_ref=mine,
                    send_sem=col_send.at[phase, d],
                    recv_sem=col_recv.at[phase, d],
                    device_id={"col": lax.rem(my_col + d, n_col)},
                )
            )
            copies[-1].start()
        sends.extend(copies)
        for copy in copies:
            copy.wait_recv()

    def exchange_row(phase, first, last):
        copies = []
        for d in range(1, n_row):
            mine = row_buf.at[phase, pl.ds(first, last - first), my_row]
            copies.append(
                pltpu.make_async_remote_copy(
                    src_ref=mine,
                    dst_ref=mine,
                    send_sem=row_send.at[phase, d],
                    recv_sem=row_recv.at[phase, d],
                    device_id={"row": lax.rem(my_row + d, n_row)},
                )
            )
            copies[-1].start()
        sends.extend(copies)
        for copy in copies:
            copy.wait_recv()

    def col_sum(phase, first, last):
        total = col_buf[phase, 0, first:last]
        for i in range(1, n_col):
            total = total + col_buf[phase, i, first:last]
        return total

    extra = bands

    def plane_sum(phase):
        total = row_buf[phase, extra, 0]
        for i in range(1, n_row):
            total = total + row_buf[phase, extra, i]
        return jnp.sum(total, axis=(0, 1), keepdims=True)

    def expand(phase, i):
        total = None
        for k in range(bands):
            at = i * bands + k
            value = row_buf[phase, at].reshape(n_row * tile, LANES)
            wide[at, 0 : n_row * tile, :] = value
            wide[at, length : length + n_row * tile, :] = value
            start = length - halves * offsets[0, k]
            part = wide[at, pl.ds(start, length), :]
            total = part if total is None else total + part
        return total

    def lines(value):
        return jnp.sum(value, axis=0, keepdims=True)

    col_phase = 0
    row_phase = 0
    forward(x_ref, col_phase)
    exchange_col(col_phase, 2 * tile)
    total = col_sum(col_phase, 0, 2 * tile)
    g, a = total[0:tile], total[tile : 2 * tile]
    col_phase += 1

    z, y = z_ref[...], y_ref[...]
    primal, dual = [], []

    def record(dual_sum):
        primal.append(jnp.max(jnp.abs(a - z), axis=0, keepdims=True))
        value = jnp.abs(d_ref[...] * x_ref[...] + q_ref[...] + dual_sum)
        dual.append(jnp.max(value, axis=0, keepdims=True))

    for outer in range(ITERS):
        vectors = [(-g, rho_step * z - y - rho_step * a)]
        if outer > 0:
            vectors.append((g, y))
        backward(vectors, row_phase)
        exchange_row(row_phase, 0, bands * len(vectors))
        start_sum = expand(row_phase, 0)
        if outer > 0:
            record(expand(row_phase, 1))
        row_phase += 1
        x = x_ref[...]
        shifted = d_ref[...] + sigma_shift
        r_ref[...] = sigma_shift * x - q_ref[...] - shifted * x + start_sum
        s_ref[...] = x
        g_s, a_s = g, a
        for inner in range(CG_STEPS):
            r = r_ref[...]
            weighted = (d_ref[...] + sigma_shift) * r
            at = 2 * tile
            used = 2 if inner == 0 else 3
            col_buf[col_phase, my_col, at : at + 1, :] = lines(r * r)
            col_buf[col_phase, my_col, at + 1 : at + 2, :] = lines(weighted * r)
            if inner > 0:
                col_buf[col_phase, my_col, at + 2 : at + 3, :] = lines(weighted * p_ref[...])
            forward(r_ref, col_phase)
            exchange_col(col_phase, at + used)
            total = col_sum(col_phase, 0, at)
            sums = jnp.sum(col_sum(col_phase, at, at + used), axis=1, keepdims=True)
            col_phase += 1
            norm, w_rem = sums[0:1], sums[1:2]
            g_r, a_r = total[0:tile], total[tile : 2 * tile]
            if inner == 0:
                p_ref[...] = r
                g_d, a_d, w_dir = g_r, a_r, w_rem
            else:
                ratio = norm / norm_old
                w_mix = sums[2:3]
                p_ref[...] = r + ratio * p_ref[...]
                g_d = g_r + ratio * g_d
                a_d = a_r + ratio * a_d
                w_dir = w_rem + 2.0 * ratio * w_mix + ratio * ratio * w_dir
            row_buf[row_phase, extra, my_row] = g_d * g_d + rho_step * (a_d * a_d)
            if inner < CG_STEPS - 1:
                backward([(g_d, rho_step * a_d)], row_phase)
                exchange_row(row_phase, 0, extra + 1)
            else:
                exchange_row(row_phase, extra, extra + 1)
            alpha = norm / (plane_sum(row_phase) + w_dir)
            p = p_ref[...]
            s_ref[...] = s_ref[...] + alpha * p
            g_s = g_s + alpha * g_d
            a_s = a_s + alpha * a_d
            if inner < CG_STEPS - 1:
                image = expand(row_phase, 0) + (d_ref[...] + sigma_shift) * p
                r_ref[...] = r_ref[...] - alpha * image
            row_phase += 1
            norm_old = norm
        x_ref[...] = relaxation * s_ref[...] + (1.0 - relaxation) * x_ref[...]
        g = relaxation * g_s + (1.0 - relaxation) * g
        a = relaxation * a_s + (1.0 - relaxation) * a
        blended = relaxation * a_s + (1.0 - relaxation) * z
        z_new = jnp.minimum(jnp.maximum(blended + y / rho_step, lower_ref[...]), upper_ref[...])
        y = y + rho_step * (blended - z_new)
        z = z_new
    z_ref[...] = z
    y_ref[...] = y

    backward([(g, y)], row_phase)
    exchange_row(row_phase, 0, bands)
    record(expand(row_phase, 0))
    row_phase += 1

    found = primal + dual
    row_buf[row_phase, extra, my_row] = jnp.zeros((tile, LANES), f32)
    for i, value in enumerate(found):
        row_buf[row_phase, extra, my_row, i : i + 1, :] = value
    exchange_row(row_phase, extra, extra + 1)
    total = row_buf[row_phase, extra, 0]
    for i in range(1, n_row):
        total = jnp.maximum(total, row_buf[row_phase, extra, i])
    col_buf[col_phase, my_col, 0:tile] = total
    exchange_col(col_phase, tile)
    total = col_buf[col_phase, 0, 0:tile]
    for i in range(1, n_col):
        total = jnp.maximum(total, col_buf[col_phase, i, 0:tile])
    top = jnp.max(total, axis=1, keepdims=True)
    for i in range(len(found)):
        u, v = divmod(i, ITERS)
        res_ref[u : u + 1, v : v + 1] = top[i : i + 1]
    for copy in sends:
        copy.wait_send()


def solution(mesh):
    n_row, n_col = mesh.shape["row"], mesh.shape["col"]

    def local(a, g, offsets, pattern, q, d, lower, upper, x, z, y):
        row_blocks, bands, bs, _ = a.shape
        tile = row_blocks * bs // LANES
        length = x.shape[0] // LANES
        planes = 2 * bands
        col_phases = 2 + ITERS * CG_STEPS
        row_phases = ITERS * (CG_STEPS + 1) + 2
        flat = lambda v: v.reshape(-1, LANES)
        vmem = pl.BlockSpec(memory_space=pltpu.VMEM)
        hbm = pl.BlockSpec(memory_space=pltpu.HBM)
        out = pl.pallas_call(
            functools.partial(kernel, n_row, n_col),
            name="osqp",
            out_shape=(
                jax.ShapeDtypeStruct((length, LANES), f32),
                jax.ShapeDtypeStruct((tile, LANES), f32),
                jax.ShapeDtypeStruct((tile, LANES), f32),
                jax.ShapeDtypeStruct((2, ITERS), f32),
            ),
            in_specs=[hbm] * 11,
            out_specs=(vmem, vmem, vmem, vmem),
            scratch_shapes=[
                pltpu.VMEM(a.shape, f32),
                pltpu.VMEM(g.shape, f32),
                pltpu.SMEM(offsets.shape, jnp.int32),
                pltpu.SMEM(pattern.shape, jnp.int32),
                pltpu.VMEM((length, LANES), f32),
                pltpu.VMEM((length, LANES), f32),
                pltpu.VMEM((tile, LANES), f32),
                pltpu.VMEM((tile, LANES), f32),
                pltpu.SemaphoreType.DMA((row_blocks, 2)),
                pltpu.SemaphoreType.DMA((9,)),
                pltpu.VMEM((row_blocks, 2 * bs, bands * bs), bf16),
                pltpu.VMEM((row_blocks, 2 * bs, bands * bs), bf16),
                pltpu.VMEM((length, LANES), f32),
                pltpu.VMEM((length, LANES), f32),
                pltpu.VMEM((length, LANES), f32),
                pltpu.VMEM((2 * bands, 2 * length, LANES), f32),
                pltpu.VMEM((col_phases, n_col, 2 * tile + 8, LANES), f32),
                pltpu.VMEM((row_phases, planes, n_row, tile, LANES), f32),
                pltpu.SemaphoreType.DMA((col_phases, n_col)),
                pltpu.SemaphoreType.DMA((col_phases, n_col)),
                pltpu.SemaphoreType.DMA((row_phases, n_row)),
                pltpu.SemaphoreType.DMA((row_phases, n_row)),
            ],
            compiler_params=pltpu.CompilerParams(
                collective_id=0, has_side_effects=True, vmem_limit_bytes=56 << 20
            ),
        )(a, g, offsets, pattern, flat(q), flat(d), flat(lower), flat(upper), flat(x), flat(z), flat(y))
        return out[0].reshape(-1), out[1].reshape(-1), out[2].reshape(-1), out[3]

    placed = (
        P("row", "col", None, None),
        P("row", "col", None, None),
        P("col", None),
        P("row", "col"),
        P("col"),
        P("col"),
        P("row"),
        P("row"),
        P("col"),
        P("row"),
        P("row"),
    )
    return jax.shard_map(
        local,
        mesh=mesh,
        in_specs=placed,
        out_specs=(P("col"), P("row"), P("row"), P()),
        check_vma=False,
    )
```

```python
import functools

import jax
import jax.numpy as jnp
from jax import lax
from jax.experimental import pallas as pl
from jax.experimental.pallas import tpu as pltpu
from jax.sharding import PartitionSpec as P

ITERS = 2
CG_STEPS = 2
LANES = 128

sigma_shift = 1e-06
rho_step = 0.1
relaxation = 1.6

f32 = jnp.float32
bf16 = jnp.bfloat16


def far_first(n):
    return sorted(range(1, n), key=lambda d: -min(d, n - d))


def hand_over(*refs):
    n = (len(refs) - 1) // 3
    sources, targets, held, sem = refs[:n], refs[n : 2 * n], refs[2 * n : 3 * n], refs[-1]
    inward = [pltpu.make_async_copy(sources[i], held[i], sem.at[0, i]) for i in range(n)]
    outward = [pltpu.make_async_copy(held[i], targets[i], sem.at[1, i]) for i in range(n)]
    for copy in inward:
        copy.start()
    for i in range(n):
        inward[i].wait()
        outward[i].start()
    for copy in outward:
        copy.wait()


def kernel(
    n_row,
    n_col,
    a_hbm,
    g_hbm,
    offsets_hbm,
    pattern_hbm,
    q_hbm,
    d_hbm,
    lower_hbm,
    upper_hbm,
    x_hbm,
    z_hbm,
    y_hbm,
    x_ref,
    z_ref,
    y_ref,
    res_ref,
    a_blocks,
    g_blocks,
    offsets,
    pattern,
    q_ref,
    d_ref,
    lower_ref,
    upper_ref,
    block_sem,
    small_sem,
    f_hi,
    f_lo,
    r_ref,
    p_ref,
    s_ref,
    wide,
    col_buf,
    row_buf,
    col_send,
    col_recv,
    row_send,
    row_recv,
):
    row_blocks, bands, bs, _ = a_blocks.shape
    halves = bs // LANES
    tile = halves * row_blocks
    length = x_ref.shape[0]
    col_blocks = length // halves
    my_row = lax.axis_index("row")
    my_col = lax.axis_index("col")

    small = [
        pltpu.make_async_copy(src, dst, small_sem.at[i])
        for i, (src, dst) in enumerate(
            (
                (pattern_hbm, pattern),
                (offsets_hbm, offsets),
                (x_hbm, x_ref),
                (z_hbm, z_ref),
                (y_hbm, y_ref),
                (q_hbm, q_ref),
                (d_hbm, d_ref),
                (lower_hbm, lower_ref),
                (upper_hbm, upper_ref),
            )
        )
    ]
    loads = [
        [
            pltpu.make_async_copy(src.at[t], dst.at[t], block_sem.at[t, m])
            for m, (src, dst) in enumerate(((g_hbm, g_blocks), (a_hbm, a_blocks)))
        ]
        for t in range(row_blocks)
    ]
    for copy in small[:2]:
        copy.start()
    for pair in loads:
        for copy in pair:
            copy.start()
    for copy in small[2:]:
        copy.start()

    barrier = pltpu.get_barrier_semaphore()
    for d in range(1, n_row):
        pl.semaphore_signal(barrier, inc=1, device_id={"row": lax.rem(my_row + d, n_row)})
    for d in range(1, n_col):
        pl.semaphore_signal(barrier, inc=1, device_id={"col": lax.rem(my_col + d, n_col)})

    wide[...] = jnp.zeros_like(wide)
    for copy in small[:2]:
        copy.wait()
    for t in range(row_blocks):
        for copy in loads[t]:
            copy.wait()
        for k in range(bands):
            on = pattern[k, t].astype(f32)
            for m, blocks in enumerate((g_blocks, a_blocks)):
                value = blocks[t, k] * on
                high = value.astype(bf16)
                f_hi[t, m * bs : (m + 1) * bs, k * bs : (k + 1) * bs] = high
                f_lo[t, m * bs : (m + 1) * bs, k * bs : (k + 1) * bs] = (
                    value - high.astype(f32)
                ).astype(bf16)
    for copy in small[2:]:
        copy.wait()
    pl.semaphore_wait(barrier, n_row + n_col - 2)

    line = lax.broadcasted_iota(jnp.int32, (8, bands * bs), 0)
    line_y = lax.broadcasted_iota(jnp.int32, (8, 2 * bs), 0)
    sends = []

    def stacked(rows, line):
        total = jnp.zeros(line.shape, f32)
        for i, value in enumerate(rows):
            high = value.astype(bf16).astype(f32)
            total = jnp.where(line == 2 * i, high, total)
            total = jnp.where(line == 2 * i + 1, value - high, total)
        return total.astype(bf16)

    def forward(ref, phase):
        for t in range(row_blocks):
            pieces = []
            for k in range(bands):
                c = lax.rem(my_row * row_blocks + t + offsets[0, k], col_blocks)
                for h in range(halves):
                    pieces.append(ref[pl.ds(c * halves + h, 1), :])
            lhs = stacked([jnp.concatenate(pieces, axis=1)], line)
            dims = (((1,), (1,)), ((), ()))
            out = lax.dot_general(lhs, f_hi[t], dims, preferred_element_type=f32)
            out = out + lax.dot_general(lhs, f_lo[t], dims, preferred_element_type=f32)
            out = out[0:1] + out[1:2]
            for m in range(2):
                for h in range(halves):
                    at = m * bs + h * LANES
                    row = m * tile + t * halves + h
                    col_buf[phase, my_col, row : row + 1, :] = out[:, at : at + LANES]

    def backward(vectors, phase):
        for t in range(row_blocks):
            rows = []
            for g, a in vectors:
                rows.append(
                    jnp.concatenate(
                        [v[t * halves + h : t * halves + h + 1] for v in (g, a) for h in range(halves)],
                        axis=1,
                    )
                )
            lhs = stacked(rows, line_y)
            out = jnp.dot(lhs, f_hi[t], preferred_element_type=f32)
            out = out + jnp.dot(lhs, f_lo[t], preferred_element_type=f32)
            for i in range(len(vectors)):
                value = out[2 * i : 2 * i + 1] + out[2 * i + 1 : 2 * i + 2]
                for k in range(bands):
                    for h in range(halves):
                        at = k * bs + h * LANES
                        row = t * halves + h
                        row_buf[phase, i * bands + k, my_row, row : row + 1, :] = value[
                            :, at : at + LANES
                        ]

    def exchange_col(phase, rows):
        copies = []
        for d in far_first(n_col):
            mine = col_buf.at[phase, my_col, pl.ds(0, rows)]
            copies.append(
                pltpu.make_async_remote_copy(
                    src_ref=mine,
                    dst_ref=mine,
                    send_sem=col_send.at[phase, d],
                    recv_sem=col_recv.at[phase, d],
                    device_id={"col": lax.rem(my_col + d, n_col)},
                )
            )
            copies[-1].start()
        sends.extend(copies)
        for copy in copies:
            copy.wait_recv()

    def exchange_row(phase, first, last):
        copies = []
        for d in far_first(n_row):
            mine = row_buf.at[phase, pl.ds(first, last - first), my_row]
            copies.append(
                pltpu.make_async_remote_copy(
                    src_ref=mine,
                    dst_ref=mine,
                    send_sem=row_send.at[phase, d],
                    recv_sem=row_recv.at[phase, d],
                    device_id={"row": lax.rem(my_row + d, n_row)},
                )
            )
            copies[-1].start()
        sends.extend(copies)
        for copy in copies:
            copy.wait_recv()

    def col_sum(phase, first, last):
        total = col_buf[phase, 0, first:last]
        for i in range(1, n_col):
            total = total + col_buf[phase, i, first:last]
        return total

    extra = bands

    def plane_sum(phase):
        total = row_buf[phase, extra, 0]
        for i in range(1, n_row):
            total = total + row_buf[phase, extra, i]
        return jnp.sum(total, axis=(0, 1), keepdims=True)

    def expand(phase, i):
        total = None
        for k in range(bands):
            at = i * bands + k
            value = row_buf[phase, at].reshape(n_row * tile, LANES)
            wide[at, 0 : n_row * tile, :] = value
            wide[at, length : length + n_row * tile, :] = value
            start = length - halves * offsets[0, k]
            part = wide[at, pl.ds(start, length), :]
            total = part if total is None else total + part
        return total

    def lines(value):
        return jnp.sum(value, axis=0, keepdims=True)

    col_phase = 0
    row_phase = 0
    forward(x_ref, col_phase)
    exchange_col(col_phase, 2 * tile)
    total = col_sum(col_phase, 0, 2 * tile)
    g, a = total[0:tile], total[tile : 2 * tile]
    col_phase += 1

    z, y = z_ref[...], y_ref[...]
    primal, dual = [], []

    def dual_max(dual_sum):
        value = jnp.abs(d_ref[...] * x_ref[...] + q_ref[...] + dual_sum)
        return jnp.max(value, axis=0, keepdims=True)

    for outer in range(ITERS):
        vectors = [(-g, rho_step * z - y - rho_step * a)]
        if outer > 0:
            vectors.append((g, y))
        backward(vectors, row_phase)
        exchange_row(row_phase, 0, bands * len(vectors))
        start_sum = expand(row_phase, 0)
        if outer > 0:
            primal.append(jnp.max(jnp.abs(a - z), axis=0, keepdims=True))
            dual.append(dual_max(expand(row_phase, 1)))
        row_phase += 1
        x = x_ref[...]
        shifted = d_ref[...] + sigma_shift
        r_ref[...] = sigma_shift * x - q_ref[...] - shifted * x + start_sum
        s_ref[...] = x
        g_s, a_s = g, a
        for inner in range(CG_STEPS):
            r = r_ref[...]
            weighted = (d_ref[...] + sigma_shift) * r
            at = 2 * tile
            used = 2 if inner == 0 else 3
            col_buf[col_phase, my_col, at : at + 1, :] = lines(r * r)
            col_buf[col_phase, my_col, at + 1 : at + 2, :] = lines(weighted * r)
            if inner > 0:
                col_buf[col_phase, my_col, at + 2 : at + 3, :] = lines(weighted * p_ref[...])
            forward(r_ref, col_phase)
            exchange_col(col_phase, at + used)
            total = col_sum(col_phase, 0, at)
            sums = jnp.sum(col_sum(col_phase, at, at + used), axis=1, keepdims=True)
            col_phase += 1
            norm, w_rem = sums[0:1], sums[1:2]
            g_r, a_r = total[0:tile], total[tile : 2 * tile]
            if inner == 0:
                p_ref[...] = r
                g_d, a_d, w_dir = g_r, a_r, w_rem
            else:
                ratio = norm / norm_old
                w_mix = sums[2:3]
                p_ref[...] = r + ratio * p_ref[...]
                g_d = g_r + ratio * g_d
                a_d = a_r + ratio * a_d
                w_dir = w_rem + 2.0 * ratio * w_mix + ratio * ratio * w_dir
            row_buf[row_phase, extra, my_row] = g_d * g_d + rho_step * (a_d * a_d)
            if inner < CG_STEPS - 1:
                backward([(g_d, rho_step * a_d)], row_phase)
                exchange_row(row_phase, 0, extra + 1)
            else:
                exchange_row(row_phase, extra, extra + 1)
            alpha = norm / (plane_sum(row_phase) + w_dir)
            p = p_ref[...]
            s_ref[...] = s_ref[...] + alpha * p
            g_s = g_s + alpha * g_d
            a_s = a_s + alpha * a_d
            if inner < CG_STEPS - 1:
                image = expand(row_phase, 0) + (d_ref[...] + sigma_shift) * p
                r_ref[...] = r_ref[...] - alpha * image
            row_phase += 1
            norm_old = norm
        x_ref[...] = relaxation * s_ref[...] + (1.0 - relaxation) * x_ref[...]
        g = relaxation * g_s + (1.0 - relaxation) * g
        a = relaxation * a_s + (1.0 - relaxation) * a
        blended = relaxation * a_s + (1.0 - relaxation) * z
        z_new = jnp.minimum(jnp.maximum(blended + y / rho_step, lower_ref[...]), upper_ref[...])
        y = y + rho_step * (blended - z_new)
        z = z_new
    z_ref[...] = z
    y_ref[...] = y

    backward([(g, y)], row_phase)
    primal.append(jnp.max(jnp.abs(a - z), axis=0, keepdims=True))
    row_buf[row_phase, extra, my_row] = jnp.zeros((tile, LANES), f32)
    for i, value in enumerate(primal):
        row_buf[row_phase, extra, my_row, i : i + 1, :] = value
    exchange_row(row_phase, 0, extra + 1)
    dual.append(dual_max(expand(row_phase, 0)))
    total = row_buf[row_phase, extra, 0]
    for i in range(1, n_row):
        total = jnp.maximum(total, row_buf[row_phase, extra, i])
    for i, value in enumerate(dual):
        col_buf[col_phase, my_col, i : i + 1, :] = value
    exchange_col(col_phase, ITERS)
    found = col_buf[col_phase, 0, 0:ITERS]
    for i in range(1, n_col):
        found = jnp.maximum(found, col_buf[col_phase, i, 0:ITERS])
    for u, value in enumerate((total[0:ITERS], found)):
        top = jnp.max(value, axis=1, keepdims=True)
        for v in range(ITERS):
            res_ref[u : u + 1, v : v + 1] = top[v : v + 1]
    for copy in sends:
        copy.wait_send()


def solution(mesh):
    n_row, n_col = mesh.shape["row"], mesh.shape["col"]

    def local(a, g, offsets, pattern, q, d, lower, upper, x, z, y):
        row_blocks, bands, bs, _ = a.shape
        tile = row_blocks * bs // LANES
        length = x.shape[0] // LANES
        planes = 2 * bands
        col_phases = 2 + ITERS * CG_STEPS
        row_phases = ITERS * (CG_STEPS + 1) + 1
        flat = lambda v: v.reshape(-1, LANES)
        vmem = pl.BlockSpec(memory_space=pltpu.VMEM)
        hbm = pl.BlockSpec(memory_space=pltpu.HBM)
        out = pl.pallas_call(
            functools.partial(kernel, n_row, n_col),
            name="osqp",
            out_shape=(
                jax.ShapeDtypeStruct((length, LANES), f32),
                jax.ShapeDtypeStruct((tile, LANES), f32),
                jax.ShapeDtypeStruct((tile, LANES), f32),
                jax.ShapeDtypeStruct((2, ITERS), f32),
            ),
            in_specs=[hbm] * 11,
            out_specs=(vmem, vmem, vmem, vmem),
            scratch_shapes=[
                pltpu.VMEM(a.shape, f32),
                pltpu.VMEM(g.shape, f32),
                pltpu.SMEM(offsets.shape, jnp.int32),
                pltpu.SMEM(pattern.shape[::-1], jnp.int32),
                pltpu.VMEM((length, LANES), f32),
                pltpu.VMEM((length, LANES), f32),
                pltpu.VMEM((tile, LANES), f32),
                pltpu.VMEM((tile, LANES), f32),
                pltpu.SemaphoreType.DMA((row_blocks, 2)),
                pltpu.SemaphoreType.DMA((9,)),
                pltpu.VMEM((row_blocks, 2 * bs, bands * bs), bf16),
                pltpu.VMEM((row_blocks, 2 * bs, bands * bs), bf16),
                pltpu.VMEM((length, LANES), f32),
                pltpu.VMEM((length, LANES), f32),
                pltpu.VMEM((length, LANES), f32),
                pltpu.VMEM((2 * bands, 2 * length, LANES), f32),
                pltpu.VMEM((col_phases, n_col, 2 * tile + 8, LANES), f32),
                pltpu.VMEM((row_phases, planes, n_row, tile, LANES), f32),
                pltpu.SemaphoreType.DMA((col_phases, n_col)),
                pltpu.SemaphoreType.DMA((col_phases, n_col)),
                pltpu.SemaphoreType.DMA((row_phases, n_row)),
                pltpu.SemaphoreType.DMA((row_phases, n_row)),
            ],
            compiler_params=pltpu.CompilerParams(
                collective_id=0, has_side_effects=True, vmem_limit_bytes=56 << 20
            ),
        )(a, g, offsets, pattern.T, flat(q), flat(d), flat(lower), flat(upper), flat(x), flat(z), flat(y))
        out = pl.pallas_call(
            hand_over,
            name="hand_over",
            out_shape=tuple(jax.ShapeDtypeStruct(v.shape, v.dtype) for v in out),
            in_specs=[hbm] * len(out),
            out_specs=(hbm,) * len(out),
            scratch_shapes=[pltpu.VMEM(v.shape, v.dtype) for v in out]
            + [pltpu.SemaphoreType.DMA((2, len(out)))],
        )(*out)
        return out[0].reshape(-1), out[1].reshape(-1), out[2].reshape(-1), out[3]

    placed = (
        P("row", "col", None, None),
        P("row", "col", None, None),
        P("col", None),
        P("row", "col"),
        P("col"),
        P("col"),
        P("row"),
        P("row"),
        P("col"),
        P("row"),
        P("row"),
    )
    return jax.shard_map(
        local,
        mesh=mesh,
        in_specs=placed,
        out_specs=(P("col"), P("row"), P("row"), P()),
        check_vma=False,
    )
```

```python
import functools

import jax
import jax.numpy as jnp
from jax import lax
from jax.experimental import pallas as pl
from jax.experimental.pallas import tpu as pltpu
from jax.sharding import PartitionSpec as P

ITERS = 2
CG_STEPS = 2
LANES = 128

sigma_shift = 1e-06
rho_step = 0.1
relaxation = 1.6

f32 = jnp.float32
bf16 = jnp.bfloat16


def far_first(n):
    return sorted(range(1, n), key=lambda d: -min(d, n - d))


def hand_over(*refs):
    n = (len(refs) - 1) // 3
    sources, targets, held, sem = refs[:n], refs[n : 2 * n], refs[2 * n : 3 * n], refs[-1]
    inward = [pltpu.make_async_copy(sources[i], held[i], sem.at[0, i]) for i in range(n)]
    outward = [pltpu.make_async_copy(held[i], targets[i], sem.at[1, i]) for i in range(n)]
    for copy in inward:
        copy.start()
    for i in range(n):
        inward[i].wait()
        outward[i].start()
    for copy in outward:
        copy.wait()


def kernel(
    n_row,
    n_col,
    a_hbm,
    g_hbm,
    offsets_hbm,
    pattern_hbm,
    q_hbm,
    d_hbm,
    lower_hbm,
    upper_hbm,
    x_hbm,
    z_hbm,
    y_hbm,
    x_ref,
    z_ref,
    y_ref,
    res_ref,
    a_blocks,
    g_blocks,
    offsets,
    pattern,
    q_ref,
    d_ref,
    lower_ref,
    upper_ref,
    block_sem,
    small_sem,
    f_hi,
    f_lo,
    r_ref,
    p_ref,
    s_ref,
    wide,
    col_buf,
    row_buf,
    col_send,
    col_recv,
    row_send,
    row_recv,
):
    row_blocks, bands, bs, _ = a_blocks.shape
    halves = bs // LANES
    tile = halves * row_blocks
    length = x_ref.shape[0]
    col_blocks = length // halves
    my_row = lax.axis_index("row")
    my_col = lax.axis_index("col")

    small = [
        pltpu.make_async_copy(src, dst, small_sem.at[i])
        for i, (src, dst) in enumerate(
            (
                (pattern_hbm, pattern),
                (offsets_hbm, offsets),
                (x_hbm, x_ref),
                (z_hbm, z_ref),
                (y_hbm, y_ref),
                (q_hbm, q_ref),
                (d_hbm, d_ref),
                (lower_hbm, lower_ref),
                (upper_hbm, upper_ref),
            )
        )
    ]
    loads = [
        [
            pltpu.make_async_copy(src.at[t], dst.at[t], block_sem.at[t, m])
            for m, (src, dst) in enumerate(((g_hbm, g_blocks), (a_hbm, a_blocks)))
        ]
        for t in range(row_blocks)
    ]
    for copy in small[:2]:
        copy.start()
    for pair in loads:
        for copy in pair:
            copy.start()
    for copy in small[2:]:
        copy.start()

    barrier = pltpu.get_barrier_semaphore()
    for d in range(1, n_row):
        pl.semaphore_signal(barrier, inc=1, device_id={"row": lax.rem(my_row + d, n_row)})
    for d in range(1, n_col):
        pl.semaphore_signal(barrier, inc=1, device_id={"col": lax.rem(my_col + d, n_col)})

    wide[...] = jnp.zeros_like(wide)
    for copy in small[:2]:
        copy.wait()
    for t in range(row_blocks):
        for copy in loads[t]:
            copy.wait()
        for k in range(bands):
            on = pattern[k, t].astype(f32)
            for m, blocks in enumerate((g_blocks, a_blocks)):
                value = blocks[t, k] * on
                high = value.astype(bf16)
                f_hi[t, m * bs : (m + 1) * bs, k * bs : (k + 1) * bs] = high
                f_lo[t, m * bs : (m + 1) * bs, k * bs : (k + 1) * bs] = (
                    value - high.astype(f32)
                ).astype(bf16)
    for copy in small[2:]:
        copy.wait()
    pl.semaphore_wait(barrier, n_row + n_col - 2)

    line = lax.broadcasted_iota(jnp.int32, (8, bands * bs), 0)
    line_y = lax.broadcasted_iota(jnp.int32, (8, 2 * bs), 0)
    sends = []

    def stacked(rows, line):
        total = jnp.zeros(line.shape, f32)
        for i, value in enumerate(rows):
            high = value.astype(bf16).astype(f32)
            total = jnp.where(line == 2 * i, high, total)
            total = jnp.where(line == 2 * i + 1, value - high, total)
        return total.astype(bf16)

    def forward(ref, phase, used):
        lhs = []
        for t in range(row_blocks):
            pieces = []
            for k in range(bands):
                c = lax.rem(my_row * row_blocks + t + offsets[0, k], col_blocks)
                for h in range(halves):
                    pieces.append(ref[pl.ds(c * halves + h, 1), :])
            lhs.append(stacked([jnp.concatenate(pieces, axis=1)], line))
        dims = (((1,), (1,)), ((), ()))
        copies = []
        for m in range(2):
            rows = []
            for t in range(row_blocks):
                high, low = (f[t, m * bs : (m + 1) * bs, :] for f in (f_hi, f_lo))
                out = lax.dot_general(lhs[t], high, dims, preferred_element_type=f32)
                out = out + lax.dot_general(lhs[t], low, dims, preferred_element_type=f32)
                out = out[0:1] + out[1:2]
                rows.extend(out[:, h * LANES : (h + 1) * LANES] for h in range(halves))
            col_buf[phase, my_col, m * tile : (m + 1) * tile, :] = jnp.concatenate(rows, axis=0)
            copies.extend(start_col(phase, m, m * tile, tile + m * used))
        for copy in copies:
            copy.wait_recv()

    def backward(vectors, phase):
        lhs = []
        for t in range(row_blocks):
            rows = []
            for g, a in vectors:
                rows.append(
                    jnp.concatenate(
                        [v[t * halves + h : t * halves + h + 1] for v in (g, a) for h in range(halves)],
                        axis=1,
                    )
                )
            lhs.append(stacked(rows, line_y))
        outs = []
        for t in range(row_blocks):
            out = jnp.dot(lhs[t], f_hi[t], preferred_element_type=f32)
            outs.append(out + jnp.dot(lhs[t], f_lo[t], preferred_element_type=f32))
        for i in range(len(vectors)):
            values = [out[2 * i : 2 * i + 1] + out[2 * i + 1 : 2 * i + 2] for out in outs]
            for k in range(bands):
                rows = []
                for value in values:
                    for h in range(halves):
                        at = k * bs + h * LANES
                        rows.append(value[:, at : at + LANES])
                row_buf[phase, i * bands + k, my_row] = jnp.concatenate(rows, axis=0)

    def start_col(phase, part, first, rows):
        copies = []
        for d in far_first(n_col):
            mine = col_buf.at[phase, my_col, pl.ds(first, rows)]
            copies.append(
                pltpu.make_async_remote_copy(
                    src_ref=mine,
                    dst_ref=mine,
                    send_sem=col_send.at[phase, part, d],
                    recv_sem=col_recv.at[phase, part, d],
                    device_id={"col": lax.rem(my_col + d, n_col)},
                )
            )
            copies[-1].start()
        sends.extend(copies)
        return copies

    def exchange_row(phase, first, last):
        copies = []
        for d in far_first(n_row):
            mine = row_buf.at[phase, pl.ds(first, last - first), my_row]
            copies.append(
                pltpu.make_async_remote_copy(
                    src_ref=mine,
                    dst_ref=mine,
                    send_sem=row_send.at[phase, d],
                    recv_sem=row_recv.at[phase, d],
                    device_id={"row": lax.rem(my_row + d, n_row)},
                )
            )
            copies[-1].start()
        sends.extend(copies)
        for copy in copies:
            copy.wait_recv()

    def col_sum(phase, first, last):
        total = col_buf[phase, 0, first:last]
        for i in range(1, n_col):
            total = total + col_buf[phase, i, first:last]
        return total

    extra = bands

    def plane_sum(phase):
        total = row_buf[phase, extra, 0]
        for i in range(1, n_row):
            total = total + row_buf[phase, extra, i]
        return jnp.sum(total, axis=(0, 1), keepdims=True)

    def expand(phase, i):
        total = None
        for k in range(bands):
            at = i * bands + k
            value = row_buf[phase, at].reshape(n_row * tile, LANES)
            wide[at, 0 : n_row * tile, :] = value
            wide[at, length : length + n_row * tile, :] = value
            start = length - halves * offsets[0, k]
            part = wide[at, pl.ds(start, length), :]
            total = part if total is None else total + part
        return total

    def lines(value):
        return jnp.sum(value, axis=0, keepdims=True)

    col_phase = 0
    row_phase = 0
    forward(x_ref, col_phase, 0)
    total = col_sum(col_phase, 0, 2 * tile)
    g, a = total[0:tile], total[tile : 2 * tile]
    col_phase += 1

    z, y = z_ref[...], y_ref[...]
    primal, dual = [], []

    def dual_max(dual_sum):
        value = jnp.abs(d_ref[...] * x_ref[...] + q_ref[...] + dual_sum)
        return jnp.max(value, axis=0, keepdims=True)

    for outer in range(ITERS):
        vectors = [(-g, rho_step * z - y - rho_step * a)]
        if outer > 0:
            vectors.append((g, y))
        backward(vectors, row_phase)
        exchange_row(row_phase, 0, bands * len(vectors))
        start_sum = expand(row_phase, 0)
        if outer > 0:
            primal.append(jnp.max(jnp.abs(a - z), axis=0, keepdims=True))
            dual.append(dual_max(expand(row_phase, 1)))
        row_phase += 1
        x = x_ref[...]
        shifted = d_ref[...] + sigma_shift
        r_ref[...] = sigma_shift * x - q_ref[...] - shifted * x + start_sum
        s_ref[...] = x
        g_s, a_s = g, a
        for inner in range(CG_STEPS):
            r = r_ref[...]
            weighted = (d_ref[...] + sigma_shift) * r
            at = 2 * tile
            used = 2 if inner == 0 else 3
            col_buf[col_phase, my_col, at : at + 1, :] = lines(r * r)
            col_buf[col_phase, my_col, at + 1 : at + 2, :] = lines(weighted * r)
            if inner > 0:
                col_buf[col_phase, my_col, at + 2 : at + 3, :] = lines(weighted * p_ref[...])
            forward(r_ref, col_phase, used)
            total = col_sum(col_phase, 0, at)
            sums = jnp.sum(col_sum(col_phase, at, at + used), axis=1, keepdims=True)
            col_phase += 1
            norm, w_rem = sums[0:1], sums[1:2]
            g_r, a_r = total[0:tile], total[tile : 2 * tile]
            if inner == 0:
                p_ref[...] = r
                g_d, a_d, w_dir = g_r, a_r, w_rem
            else:
                ratio = norm / norm_old
                w_mix = sums[2:3]
                p_ref[...] = r + ratio * p_ref[...]
                g_d = g_r + ratio * g_d
                a_d = a_r + ratio * a_d
                w_dir = w_rem + 2.0 * ratio * w_mix + ratio * ratio * w_dir
            row_buf[row_phase, extra, my_row] = g_d * g_d + rho_step * (a_d * a_d)
            if inner < CG_STEPS - 1:
                backward([(g_d, rho_step * a_d)], row_phase)
                exchange_row(row_phase, 0, extra + 1)
            else:
                exchange_row(row_phase, extra, extra + 1)
            alpha = norm / (plane_sum(row_phase) + w_dir)
            p = p_ref[...]
            s_ref[...] = s_ref[...] + alpha * p
            g_s = g_s + alpha * g_d
            a_s = a_s + alpha * a_d
            if inner < CG_STEPS - 1:
                image = expand(row_phase, 0) + (d_ref[...] + sigma_shift) * p
                r_ref[...] = r_ref[...] - alpha * image
            row_phase += 1
            norm_old = norm
        x_ref[...] = relaxation * s_ref[...] + (1.0 - relaxation) * x_ref[...]
        g = relaxation * g_s + (1.0 - relaxation) * g
        a = relaxation * a_s + (1.0 - relaxation) * a
        blended = relaxation * a_s + (1.0 - relaxation) * z
        z_new = jnp.minimum(jnp.maximum(blended + y / rho_step, lower_ref[...]), upper_ref[...])
        y = y + rho_step * (blended - z_new)
        z = z_new
    z_ref[...] = z
    y_ref[...] = y

    backward([(g, y)], row_phase)
    primal.append(jnp.max(jnp.abs(a - z), axis=0, keepdims=True))
    row_buf[row_phase, extra, my_row] = jnp.zeros((tile, LANES), f32)
    for i, value in enumerate(primal):
        row_buf[row_phase, extra, my_row, i : i + 1, :] = value
    exchange_row(row_phase, 0, extra + 1)
    dual.append(dual_max(expand(row_phase, 0)))
    total = row_buf[row_phase, extra, 0]
    for i in range(1, n_row):
        total = jnp.maximum(total, row_buf[row_phase, extra, i])
    for i, value in enumerate(dual):
        col_buf[col_phase, my_col, i : i + 1, :] = value
    for copy in start_col(col_phase, 0, 0, ITERS):
        copy.wait_recv()
    found = col_buf[col_phase, 0, 0:ITERS]
    for i in range(1, n_col):
        found = jnp.maximum(found, col_buf[col_phase, i, 0:ITERS])
    for u, value in enumerate((total[0:ITERS], found)):
        top = jnp.max(value, axis=1, keepdims=True)
        for v in range(ITERS):
            res_ref[u : u + 1, v : v + 1] = top[v : v + 1]
    for copy in sends:
        copy.wait_send()


def solution(mesh):
    n_row, n_col = mesh.shape["row"], mesh.shape["col"]

    def local(a, g, offsets, pattern, q, d, lower, upper, x, z, y):
        row_blocks, bands, bs, _ = a.shape
        tile = row_blocks * bs // LANES
        length = x.shape[0] // LANES
        planes = 2 * bands
        col_phases = 2 + ITERS * CG_STEPS
        row_phases = ITERS * (CG_STEPS + 1) + 1
        flat = lambda v: v.reshape(-1, LANES)
        vmem = pl.BlockSpec(memory_space=pltpu.VMEM)
        hbm = pl.BlockSpec(memory_space=pltpu.HBM)
        out = pl.pallas_call(
            functools.partial(kernel, n_row, n_col),
            name="osqp",
            out_shape=(
                jax.ShapeDtypeStruct((length, LANES), f32),
                jax.ShapeDtypeStruct((tile, LANES), f32),
                jax.ShapeDtypeStruct((tile, LANES), f32),
                jax.ShapeDtypeStruct((2, ITERS), f32),
            ),
            in_specs=[hbm] * 11,
            out_specs=(vmem, vmem, vmem, vmem),
            scratch_shapes=[
                pltpu.VMEM(a.shape, f32),
                pltpu.VMEM(g.shape, f32),
                pltpu.SMEM(offsets.shape, jnp.int32),
                pltpu.SMEM(pattern.shape[::-1], jnp.int32),
                pltpu.VMEM((length, LANES), f32),
                pltpu.VMEM((length, LANES), f32),
                pltpu.VMEM((tile, LANES), f32),
                pltpu.VMEM((tile, LANES), f32),
                pltpu.SemaphoreType.DMA((row_blocks, 2)),
                pltpu.SemaphoreType.DMA((9,)),
                pltpu.VMEM((row_blocks, 2 * bs, bands * bs), bf16),
                pltpu.VMEM((row_blocks, 2 * bs, bands * bs), bf16),
                pltpu.VMEM((length, LANES), f32),
                pltpu.VMEM((length, LANES), f32),
                pltpu.VMEM((length, LANES), f32),
                pltpu.VMEM((2 * bands, 2 * length, LANES), f32),
                pltpu.VMEM((col_phases, n_col, 2 * tile + 8, LANES), f32),
                pltpu.VMEM((row_phases, planes, n_row, tile, LANES), f32),
                pltpu.SemaphoreType.DMA((col_phases, 2, n_col)),
                pltpu.SemaphoreType.DMA((col_phases, 2, n_col)),
                pltpu.SemaphoreType.DMA((row_phases, n_row)),
                pltpu.SemaphoreType.DMA((row_phases, n_row)),
            ],
            compiler_params=pltpu.CompilerParams(
                collective_id=0, has_side_effects=True, vmem_limit_bytes=56 << 20
            ),
        )(a, g, offsets, pattern.T, flat(q), flat(d), flat(lower), flat(upper), flat(x), flat(z), flat(y))
        out = pl.pallas_call(
            hand_over,
            name="hand_over",
            out_shape=tuple(jax.ShapeDtypeStruct(v.shape, v.dtype) for v in out),
            in_specs=[hbm] * len(out),
            out_specs=(hbm,) * len(out),
            scratch_shapes=[pltpu.VMEM(v.shape, v.dtype) for v in out]
            + [pltpu.SemaphoreType.DMA((2, len(out)))],
        )(*out)
        return out[0].reshape(-1), out[1].reshape(-1), out[2].reshape(-1), out[3]

    placed = (
        P("row", "col", None, None),
        P("row", "col", None, None),
        P("col", None),
        P("row", "col"),
        P("col"),
        P("col"),
        P("row"),
        P("row"),
        P("col"),
        P("row"),
        P("row"),
    )
    return jax.shard_map(
        local,
        mesh=mesh,
        in_specs=placed,
        out_specs=(P("col"), P("row"), P("row"), P()),
        check_vma=False,
    )
```

```python
import functools

import jax
import jax.numpy as jnp
from jax import lax
from jax.experimental import pallas as pl
from jax.experimental.pallas import tpu as pltpu
from jax.sharding import PartitionSpec as P

ITERS = 2
CG_STEPS = 2
LANES = 128

sigma_shift = 1e-06
rho_step = 0.1
relaxation = 1.6

f32 = jnp.float32
bf16 = jnp.bfloat16


def far_first(n):
    return sorted(range(1, n), key=lambda d: -min(d, n - d))


def hand_over(*refs):
    n = (len(refs) - 1) // 3
    sources, targets, held, sem = refs[:n], refs[n : 2 * n], refs[2 * n : 3 * n], refs[-1]
    inward = [pltpu.make_async_copy(sources[i], held[i], sem.at[0, i]) for i in range(n)]
    outward = [pltpu.make_async_copy(held[i], targets[i], sem.at[1, i]) for i in range(n)]
    for copy in inward:
        copy.start()
    for i in range(n):
        inward[i].wait()
        outward[i].start()
    for copy in outward:
        copy.wait()


def kernel(
    n_row,
    n_col,
    a_hbm,
    g_hbm,
    offsets_hbm,
    pattern_hbm,
    q_hbm,
    d_hbm,
    lower_hbm,
    upper_hbm,
    x_hbm,
    z_hbm,
    y_hbm,
    x_ref,
    z_ref,
    y_ref,
    res_ref,
    a_blocks,
    g_blocks,
    offsets,
    pattern,
    q_ref,
    d_ref,
    lower_ref,
    upper_ref,
    block_sem,
    small_sem,
    f_hi,
    f_lo,
    r_ref,
    p_ref,
    s_ref,
    wide,
    col_buf,
    row_buf,
    col_send,
    col_recv,
    row_send,
    row_recv,
):
    row_blocks, bands, bs, _ = a_blocks.shape
    halves = bs // LANES
    tile = halves * row_blocks
    length = x_ref.shape[0]
    col_blocks = length // halves
    my_row = lax.axis_index("row")
    my_col = lax.axis_index("col")

    small = [
        pltpu.make_async_copy(src, dst, small_sem.at[i])
        for i, (src, dst) in enumerate(
            (
                (pattern_hbm, pattern),
                (offsets_hbm, offsets),
                (x_hbm, x_ref),
                (z_hbm, z_ref),
                (y_hbm, y_ref),
                (q_hbm, q_ref),
                (d_hbm, d_ref),
                (lower_hbm, lower_ref),
                (upper_hbm, upper_ref),
            )
        )
    ]
    loads = [
        [
            pltpu.make_async_copy(src.at[t], dst.at[t], block_sem.at[t, m])
            for m, (src, dst) in enumerate(((g_hbm, g_blocks), (a_hbm, a_blocks)))
        ]
        for t in range(row_blocks)
    ]
    for copy in small[:2]:
        copy.start()
    for pair in loads:
        for copy in pair:
            copy.start()
    for copy in small[2:]:
        copy.start()

    barrier = pltpu.get_barrier_semaphore()
    for d in range(1, n_row):
        pl.semaphore_signal(barrier, inc=1, device_id={"row": lax.rem(my_row + d, n_row)})
    for d in range(1, n_col):
        pl.semaphore_signal(barrier, inc=1, device_id={"col": lax.rem(my_col + d, n_col)})

    wide[...] = jnp.zeros_like(wide)
    for copy in small[:2]:
        copy.wait()
    for t in range(row_blocks):
        for copy in loads[t]:
            copy.wait()
        for k in range(bands):
            on = pattern[k, t].astype(f32)
            for m, blocks in enumerate((g_blocks, a_blocks)):
                value = blocks[t, k] * on
                high = value.astype(bf16)
                f_hi[t, m * bs : (m + 1) * bs, k * bs : (k + 1) * bs] = high
                f_lo[t, m * bs : (m + 1) * bs, k * bs : (k + 1) * bs] = (
                    value - high.astype(f32)
                ).astype(bf16)
    for copy in small[2:]:
        copy.wait()
    pl.semaphore_wait(barrier, n_row + n_col - 2)

    line = lax.broadcasted_iota(jnp.int32, (8, bands * bs), 0)
    line_y = lax.broadcasted_iota(jnp.int32, (8, 2 * bs), 0)
    sends = []

    def stacked(rows, line):
        total = jnp.zeros(line.shape, f32)
        for i, value in enumerate(rows):
            high = value.astype(bf16).astype(f32)
            total = jnp.where(line == 2 * i, high, total)
            total = jnp.where(line == 2 * i + 1, value - high, total)
        return total.astype(bf16)

    def forward(ref, phase, used):
        lhs = []
        for t in range(row_blocks):
            pieces = []
            for k in range(bands):
                c = lax.rem(my_row * row_blocks + t + offsets[0, k], col_blocks)
                for h in range(halves):
                    pieces.append(ref[pl.ds(c * halves + h, 1), :])
            lhs.append(stacked([jnp.concatenate(pieces, axis=1)], line))
        dims = (((1,), (1,)), ((), ()))
        for m in range(2):
            rows = []
            for t in range(row_blocks):
                high, low = (f[t, m * bs : (m + 1) * bs, :] for f in (f_hi, f_lo))
                out = lax.dot_general(lhs[t], high, dims, preferred_element_type=f32)
                out = out + lax.dot_general(lhs[t], low, dims, preferred_element_type=f32)
                out = out[0:1] + out[1:2]
                rows.extend(out[:, h * LANES : (h + 1) * LANES] for h in range(halves))
            col_buf[phase, my_col, m * tile : (m + 1) * tile, :] = jnp.concatenate(rows, axis=0)
        for copy in start_col(phase, 0, 0, 2 * tile + used):
            copy.wait_recv()

    def backward(vectors, phase):
        lhs = []
        for t in range(row_blocks):
            rows = []
            for g, a in vectors:
                rows.append(
                    jnp.concatenate(
                        [v[t * halves + h : t * halves + h + 1] for v in (g, a) for h in range(halves)],
                        axis=1,
                    )
                )
            lhs.append(stacked(rows, line_y))
        outs = []
        for t in range(row_blocks):
            out = jnp.dot(lhs[t], f_hi[t], preferred_element_type=f32)
            outs.append(out + jnp.dot(lhs[t], f_lo[t], preferred_element_type=f32))
        for i in range(len(vectors)):
            values = [out[2 * i : 2 * i + 1] + out[2 * i + 1 : 2 * i + 2] for out in outs]
            for k in range(bands):
                rows = []
                for value in values:
                    for h in range(halves):
                        at = k * bs + h * LANES
                        rows.append(value[:, at : at + LANES])
                row_buf[phase, i * bands + k, my_row] = jnp.concatenate(rows, axis=0)

    def start_col(phase, part, first, rows):
        copies = []
        for d in far_first(n_col):
            mine = col_buf.at[phase, my_col, pl.ds(first, rows)]
            copies.append(
                pltpu.make_async_remote_copy(
                    src_ref=mine,
                    dst_ref=mine,
                    send_sem=col_send.at[phase, part, d],
                    recv_sem=col_recv.at[phase, part, d],
                    device_id={"col": lax.rem(my_col + d, n_col)},
                )
            )
            copies[-1].start()
        sends.extend(copies)
        return copies

    def start_row(phase, first, last, part=0):
        copies = []
        for d in far_first(n_row):
            mine = row_buf.at[phase, pl.ds(first, last - first), my_row]
            copies.append(
                pltpu.make_async_remote_copy(
                    src_ref=mine,
                    dst_ref=mine,
                    send_sem=row_send.at[phase, part, d],
                    recv_sem=row_recv.at[phase, part, d],
                    device_id={"row": lax.rem(my_row + d, n_row)},
                )
            )
            copies[-1].start()
        sends.extend(copies)
        return copies

    def exchange_row(phase, first, last):
        for copy in start_row(phase, first, last):
            copy.wait_recv()

    def col_sum(phase, first, last):
        total = col_buf[phase, 0, first:last]
        for i in range(1, n_col):
            total = total + col_buf[phase, i, first:last]
        return total

    extra = bands

    def plane_sum(phase):
        total = row_buf[phase, extra, 0]
        for i in range(1, n_row):
            total = total + row_buf[phase, extra, i]
        return jnp.sum(total, axis=(0, 1), keepdims=True)

    def expand(phase, i):
        total = None
        for k in range(bands):
            at = i * bands + k
            value = row_buf[phase, at].reshape(n_row * tile, LANES)
            wide[at, 0 : n_row * tile, :] = value
            wide[at, length : length + n_row * tile, :] = value
            start = length - halves * offsets[0, k]
            part = wide[at, pl.ds(start, length), :]
            total = part if total is None else total + part
        return total

    def lines(value):
        return jnp.sum(value, axis=0, keepdims=True)

    col_phase = 0
    row_phase = 0
    forward(x_ref, col_phase, 0)
    total = col_sum(col_phase, 0, 2 * tile)
    g, a = total[0:tile], total[tile : 2 * tile]
    col_phase += 1

    z, y = z_ref[...], y_ref[...]
    primal, dual = [], []

    def dual_max(dual_sum):
        value = jnp.abs(d_ref[...] * x_ref[...] + q_ref[...] + dual_sum)
        return jnp.max(value, axis=0, keepdims=True)

    for outer in range(ITERS):
        vectors = [(-g, rho_step * z - y - rho_step * a)]
        if outer > 0:
            vectors.append((g, y))
        backward(vectors, row_phase)
        now = start_row(row_phase, 0, bands)
        if outer > 0:
            later = (start_row(row_phase, bands, 2 * bands, 1), row_phase)
            primal.append(jnp.max(jnp.abs(a - z), axis=0, keepdims=True))
        for copy in now:
            copy.wait_recv()
        start_sum = expand(row_phase, 0)
        row_phase += 1
        x = x_ref[...]
        shifted = d_ref[...] + sigma_shift
        r_ref[...] = sigma_shift * x - q_ref[...] - shifted * x + start_sum
        s_ref[...] = x
        g_s, a_s = g, a
        for inner in range(CG_STEPS):
            r = r_ref[...]
            weighted = (d_ref[...] + sigma_shift) * r
            at = 2 * tile
            used = 2 if inner == 0 else 3
            col_buf[col_phase, my_col, at : at + 1, :] = lines(r * r)
            col_buf[col_phase, my_col, at + 1 : at + 2, :] = lines(weighted * r)
            if inner > 0:
                col_buf[col_phase, my_col, at + 2 : at + 3, :] = lines(weighted * p_ref[...])
            forward(r_ref, col_phase, used)
            total = col_sum(col_phase, 0, at)
            sums = jnp.sum(col_sum(col_phase, at, at + used), axis=1, keepdims=True)
            col_phase += 1
            norm, w_rem = sums[0:1], sums[1:2]
            g_r, a_r = total[0:tile], total[tile : 2 * tile]
            if inner == 0:
                p_ref[...] = r
                g_d, a_d, w_dir = g_r, a_r, w_rem
            else:
                ratio = norm / norm_old
                w_mix = sums[2:3]
                p_ref[...] = r + ratio * p_ref[...]
                g_d = g_r + ratio * g_d
                a_d = a_r + ratio * a_d
                w_dir = w_rem + 2.0 * ratio * w_mix + ratio * ratio * w_dir
            row_buf[row_phase, extra, my_row] = g_d * g_d + rho_step * (a_d * a_d)
            if inner < CG_STEPS - 1:
                backward([(g_d, rho_step * a_d)], row_phase)
                exchange_row(row_phase, 0, extra + 1)
            else:
                now = start_row(row_phase, extra, extra + 1)
                if outer > 0:
                    for copy in later[0]:
                        copy.wait_recv()
                    dual.append(dual_max(expand(later[1], 1)))
                for copy in now:
                    copy.wait_recv()
            alpha = norm / (plane_sum(row_phase) + w_dir)
            p = p_ref[...]
            s_ref[...] = s_ref[...] + alpha * p
            g_s = g_s + alpha * g_d
            a_s = a_s + alpha * a_d
            if inner < CG_STEPS - 1:
                image = expand(row_phase, 0) + (d_ref[...] + sigma_shift) * p
                r_ref[...] = r_ref[...] - alpha * image
            row_phase += 1
            norm_old = norm
        x_ref[...] = relaxation * s_ref[...] + (1.0 - relaxation) * x_ref[...]
        g = relaxation * g_s + (1.0 - relaxation) * g
        a = relaxation * a_s + (1.0 - relaxation) * a
        blended = relaxation * a_s + (1.0 - relaxation) * z
        z_new = jnp.minimum(jnp.maximum(blended + y / rho_step, lower_ref[...]), upper_ref[...])
        y = y + rho_step * (blended - z_new)
        z = z_new
    z_ref[...] = z
    y_ref[...] = y

    backward([(g, y)], row_phase)
    primal.append(jnp.max(jnp.abs(a - z), axis=0, keepdims=True))
    row_buf[row_phase, extra, my_row] = jnp.zeros((tile, LANES), f32)
    for i, value in enumerate(primal):
        row_buf[row_phase, extra, my_row, i : i + 1, :] = value
    exchange_row(row_phase, 0, extra + 1)
    dual.append(dual_max(expand(row_phase, 0)))
    total = row_buf[row_phase, extra, 0]
    for i in range(1, n_row):
        total = jnp.maximum(total, row_buf[row_phase, extra, i])
    for i, value in enumerate(dual):
        col_buf[col_phase, my_col, i : i + 1, :] = value
    for copy in start_col(col_phase, 0, 0, ITERS):
        copy.wait_recv()
    found = col_buf[col_phase, 0, 0:ITERS]
    for i in range(1, n_col):
        found = jnp.maximum(found, col_buf[col_phase, i, 0:ITERS])
    for u, value in enumerate((total[0:ITERS], found)):
        top = jnp.max(value, axis=1, keepdims=True)
        for v in range(ITERS):
            res_ref[u : u + 1, v : v + 1] = top[v : v + 1]
    for copy in sends:
        copy.wait_send()


def solution(mesh):
    n_row, n_col = mesh.shape["row"], mesh.shape["col"]

    def local(a, g, offsets, pattern, q, d, lower, upper, x, z, y):
        row_blocks, bands, bs, _ = a.shape
        tile = row_blocks * bs // LANES
        length = x.shape[0] // LANES
        planes = 2 * bands
        col_phases = 2 + ITERS * CG_STEPS
        row_phases = ITERS * (CG_STEPS + 1) + 1
        flat = lambda v: v.reshape(-1, LANES)
        vmem = pl.BlockSpec(memory_space=pltpu.VMEM)
        hbm = pl.BlockSpec(memory_space=pltpu.HBM)
        out = pl.pallas_call(
            functools.partial(kernel, n_row, n_col),
            name="osqp",
            out_shape=(
                jax.ShapeDtypeStruct((length, LANES), f32),
                jax.ShapeDtypeStruct((tile, LANES), f32),
                jax.ShapeDtypeStruct((tile, LANES), f32),
                jax.ShapeDtypeStruct((2, ITERS), f32),
            ),
            in_specs=[hbm] * 11,
            out_specs=(vmem, vmem, vmem, vmem),
            scratch_shapes=[
                pltpu.VMEM(a.shape, f32),
                pltpu.VMEM(g.shape, f32),
                pltpu.SMEM(offsets.shape, jnp.int32),
                pltpu.SMEM(pattern.shape[::-1], jnp.int32),
                pltpu.VMEM((length, LANES), f32),
                pltpu.VMEM((length, LANES), f32),
                pltpu.VMEM((tile, LANES), f32),
                pltpu.VMEM((tile, LANES), f32),
                pltpu.SemaphoreType.DMA((row_blocks, 2)),
                pltpu.SemaphoreType.DMA((9,)),
                pltpu.VMEM((row_blocks, 2 * bs, bands * bs), bf16),
                pltpu.VMEM((row_blocks, 2 * bs, bands * bs), bf16),
                pltpu.VMEM((length, LANES), f32),
                pltpu.VMEM((length, LANES), f32),
                pltpu.VMEM((length, LANES), f32),
                pltpu.VMEM((2 * bands, 2 * length, LANES), f32),
                pltpu.VMEM((col_phases, n_col, 2 * tile + 8, LANES), f32),
                pltpu.VMEM((row_phases, planes, n_row, tile, LANES), f32),
                pltpu.SemaphoreType.DMA((col_phases, 2, n_col)),
                pltpu.SemaphoreType.DMA((col_phases, 2, n_col)),
                pltpu.SemaphoreType.DMA((row_phases, 2, n_row)),
                pltpu.SemaphoreType.DMA((row_phases, 2, n_row)),
            ],
            compiler_params=pltpu.CompilerParams(
                collective_id=0, has_side_effects=True, vmem_limit_bytes=56 << 20
            ),
        )(a, g, offsets, pattern.T, flat(q), flat(d), flat(lower), flat(upper), flat(x), flat(z), flat(y))
        out = pl.pallas_call(
            hand_over,
            name="hand_over",
            out_shape=tuple(jax.ShapeDtypeStruct(v.shape, v.dtype) for v in out),
            in_specs=[hbm] * len(out),
            out_specs=(hbm,) * len(out),
            scratch_shapes=[pltpu.VMEM(v.shape, v.dtype) for v in out]
            + [pltpu.SemaphoreType.DMA((2, len(out)))],
        )(*out)
        return out[0].reshape(-1), out[1].reshape(-1), out[2].reshape(-1), out[3]

    placed = (
        P("row", "col", None, None),
        P("row", "col", None, None),
        P("col", None),
        P("row", "col"),
        P("col"),
        P("col"),
        P("row"),
        P("row"),
        P("col"),
        P("row"),
        P("row"),
    )
    return jax.shard_map(
        local,
        mesh=mesh,
        in_specs=placed,
        out_specs=(P("col"), P("row"), P("row"), P()),
        check_vma=False,
    )
```
